128 devices in a mesh: adapter: 32 (over y, x, core), mp: 4 (over z).
Axes of the slice: x: 4, y: 4, z: 4, core: 2. Of those that a mesh axis runs over, the one named last changes fastest.
Arguments:
- hidden: bfloat16 [8192, 4096], P('adapter', 'mp'), may hold values from -8 to 8
- subsets: int32 [8192, 8], P('adapter'), may hold values from 0 to 31, all different within a row; in each aligned block of 256 rows (0 to 255, 256 to 511, ...) at most 128 rows name the same one
- down_weight: bfloat16 [32, 4096, 256], P('adapter', 'mp'), may hold values from -0.09375 to 0.09375
- up_weight: bfloat16 [32, 256, 4096], P('adapter', None, 'mp'), may hold values from -0.375 to 0.375
- query_weight: bfloat16 [4096, 4096], P('mp'), may hold values from -0.08 to 2.08
- key_weight: bfloat16 [4096, 4096], P('mp'), may hold values from -0.08 to 2.08
Outputs:
- joined: bfloat16 [8192, 4096], P('adapter', 'mp')
The draws below stay inside these ranges and needn't reach their ends.
Inputs may be any that keep to these rules, and one draw needn't show every extreme that they name: `subsets`: each row names 8 different adapters; within the rows of one index of the adapter axis no adapter is named by more than 128 rows.
All inputs are finite; a program needn't handle non-finite values.
Results may differ from the reference program's by a relative error of at most 0.025.
Values may be sent and summed in bfloat16 or wider, within the bound.
No kernel may reach another device: no remote copies, remote signals or barrier semaphores. Data moves between devices by JAX's collectives and lax.ppermute only.
A program may use at most 192 MiB of HBM per device.

```python
import math
import jax
import jax.numpy as jnp
import numpy as np
from jax import lax

D = 4096
B = 256
K = 8
REQ_DEV = 256
ADAPTERS = 32
REQUESTS = 8192
CAP = 128


def draw_hidden(key, part):
    values = jnp.clip(jax.random.normal(key, (REQUESTS, D), jnp.float32), -5.0, 5.0)
    return values.astype(jnp.bfloat16)


def draw_query_weight(key, part):
    values = jnp.clip(jax.random.normal(jax.random.fold_in(key, 11), (D, D), jnp.float32) * D ** (-0.5), -0.078125, 0.078125)
    return values.astype(jnp.bfloat16)


def draw_key_weight(key, part):
    values = jnp.clip(jax.random.normal(jax.random.fold_in(key, 13), (D, D), jnp.float32) * D ** (-0.5), -0.078125, 0.078125)
    return values.astype(jnp.bfloat16)


def level_of(rng, extent, pieces, least, high):
    gain = 1.0
    for axis_at, parts in pieces:
        draws = jax.random.uniform(jax.random.fold_in(jax.random.fold_in(rng, 6), axis_at), (parts,), jnp.float32, least / len(pieces), high / len(pieces))
        gain = gain * jnp.repeat(jnp.exp(draws), extent[axis_at] // parts).reshape((-1,) + (1,) * (len(extent) - 1 - axis_at))
    return gain


def shared_out(stream_key, own, number, rows, count, top, reach, lean):
    ranking = jax.random.permutation(stream_key, count)
    crowded, common = shares(count, rows * top, reach, lean, True), shares(count, rows * top, reach, lean, False)
    places = jnp.arange(count)

    def named(tallies, offset_by):
        used = int((tallies > 0).sum())
        fixed = max(1, used // 4)
        moved = fixed + (places - fixed + offset_by * (used - fixed)) % max(1, count - fixed)
        return jnp.zeros((count,), jnp.int32).at[ranking[jnp.where(places < fixed, places, moved)]].set(jnp.asarray(tallies, jnp.int32))

    tallies = jnp.where(number % 4 == 0, named(crowded, number // 4), named(common, number - number // 4 - 1))
    mixed = jax.random.permutation(jax.random.fold_in(own, 3), count)
    source_of, receiver = mixed[0:count // 2 * 2:2], mixed[1:count // 2 * 2:2]
    slack = jnp.minimum(tallies[source_of] - 1, reach - tallies[receiver]) // 2
    slack = jnp.where((source_of == ranking[0]) | (receiver == ranking[0]) | (tallies[receiver] == 0), 0, jnp.maximum(slack, 0))
    moved = jax.random.randint(jax.random.fold_in(own, 4), (count // 2,), 0, 1 << 20) % (slack + 1)
    tallies = tallies.at[source_of].add(-moved).at[receiver].add(moved)
    items = jnp.searchsorted(jnp.cumsum(tallies), jnp.arange(rows * top), side="right").astype(jnp.int32)
    table = items.reshape(top, rows).T
    table = table[jax.random.permutation(jax.random.fold_in(own, 1), rows)]
    offset_by = jax.random.randint(jax.random.fold_in(own, 2), (rows, 1), 0, top)
    return jnp.take_along_axis(table, (jnp.arange(top)[None, :] + offset_by) % top, axis=1)


def shares(number_of, total, bound, slope, full):
    weights = [(1 << 20) // math.isqrt(rank ** slope) + 1 for rank in range(1, number_of + 1)]
    largest = bound if full else min(bound, max(-(-total // number_of), total * weights[0] // sum(weights)))
    least = 1 if total - largest >= number_of - 1 else 0
    counts, surplus = [largest] + [least] * (number_of - 1), total - largest - least * (number_of - 1)
    while surplus > 0:
        candidates = [i for i in range(1, number_of) if counts[i] < largest] or [i for i in range(1, number_of) if counts[i] < bound]
        mass, left = sum([weights[i] for i in candidates]), surplus
        for i in candidates:
            extra = min(bound - counts[i], max(1, left * weights[i] // mass), surplus)
            counts[i] = counts[i] + extra
            surplus = surplus - extra
    return np.array(counts)


def bell_draw(rng, extent, spread, limit, pieces=(), kind=jnp.bfloat16):
    result = spread * jax.random.normal(rng, extent, jnp.float32)
    if pieces:
        result = result * level_of(rng, extent, pieces, -0.22, 0.18)
    return jnp.clip(result, -limit, limit).astype(kind)


def setup_inputs(seed: int = 0) -> dict:
    seeds = jax.random.split(jax.random.key(seed), 7)
    hidden = draw_hidden(jax.random.fold_in(seeds[6], 71), 0)
    subsets_keys = jax.random.split(jax.random.fold_in(seeds[1], 1), REQUESTS // REQ_DEV)
    subsets_turns = jax.random.permutation(jax.random.fold_in(seeds[1], 3), REQUESTS // REQ_DEV)
    subsets = jax.vmap(lambda own, number: shared_out(jax.random.fold_in(seeds[1], 2), own, number, REQ_DEV, ADAPTERS, K, CAP, 2))(subsets_keys, subsets_turns).reshape((REQUESTS, K))
    down_weight = bell_draw(seeds[2], (ADAPTERS, D, B), D ** -0.5, 0.09375, ((0, 32), (1, 4)))
    up_weight = bell_draw(seeds[3], (ADAPTERS, B, D), B ** -0.5, 0.375, ((0, 32), (2, 4)))
    query_weight = draw_query_weight(jax.random.fold_in(seeds[6], 71), 0)
    key_weight = draw_key_weight(jax.random.fold_in(seeds[6], 71), 0)
    return dict(hidden=hidden, subsets=subsets, down_weight=down_weight, up_weight=up_weight, query_weight=query_weight, key_weight=key_weight)


def reference(hidden, subsets, down_weight, up_weight, query_weight, key_weight):
    query = jnp.dot(hidden, query_weight, preferred_element_type=jnp.float32).astype(jnp.bfloat16)
    probe = lax.dot_general(query, key_weight, (((1,), (1,)), ((), ())), preferred_element_type=jnp.float32).astype(jnp.bfloat16)

    def visit(gathered, operands):
        index, down_one, up_one = operands
        bottle = jnp.maximum(jnp.dot(hidden, down_one, preferred_element_type=jnp.float32), 0.0).astype(jnp.bfloat16)
        produced = jnp.dot(bottle, up_one, preferred_element_type=jnp.float32).astype(jnp.bfloat16)
        landed = subsets == index
        gathered = jnp.where(landed[:, :, None], produced[:, None, :], gathered)
        return gathered, None

    start_value = jnp.zeros((REQUESTS, K, D), jnp.bfloat16)
    picked, _ = lax.scan(visit, start_value, (jnp.arange(ADAPTERS, dtype=jnp.int32), down_weight, up_weight))
    widened = picked.astype(jnp.float32)
    base = hidden.astype(jnp.float32)
    probe_wide = probe.astype(jnp.float32)
    own_term = jnp.sum(base * probe_wide, axis=1)
    logits = (jnp.einsum("rkd,rd->rk", widened, probe_wide, precision=lax.Precision.HIGHEST) + own_term[:, None]) * (D ** -0.5)
    share = jax.nn.softmax(logits, axis=-1)
    joined = base + jnp.einsum("rk,rkd->rd", share, widened, precision=lax.Precision.HIGHEST)
    return joined.astype(jnp.bfloat16)
```

```python
import jax
import jax.numpy as jnp
from jax import lax
from jax.experimental import pallas as pl
from jax.experimental.pallas import tpu as pltpu
from jax.sharding import Mesh, PartitionSpec as P

D = 4096
ADAPTERS = 32
B = 256
CAP = 128
ROWS = 256
WIDTH = 1024
TILE = 16
PAIRS = 2560
PIECE = PAIRS // 4
BUF = PAIRS + CAP
BF16 = jnp.bfloat16
F32 = jnp.float32
VMEM = 56 * 1024 * 1024


def params(**kw):
    return pltpu.CompilerParams(vmem_limit_bytes=VMEM, **kw)


def dot(a, b, ca, cb):
    return lax.dot_general(a, b, (((ca,), (cb,)), ((), ())), preferred_element_type=F32)


def iota(shape, dim):
    return lax.broadcasted_iota(jnp.int32, shape, dim)


def whole():
    return pl.BlockSpec(memory_space=pltpu.VMEM)


def plan_kernel(sub_ref, hid_ref, ext_ref, rank_ref, off_ref):
    ids = iota((ADAPTERS, ROWS), 0)
    chosen = jnp.zeros((ADAPTERS, ROWS), F32)
    for k in range(sub_ref.shape[0]):
        chosen = chosen + jnp.where(sub_ref[k : k + 1, :] == ids, 1.0, 0.0)
    named = chosen.astype(BF16)
    earlier = jnp.where(iota((ROWS, ROWS), 0) < iota((ROWS, ROWS), 1), 1.0, 0.0)
    before = dot(named, earlier.astype(BF16), 1, 0)
    rank = jnp.where(chosen > 0.5, before, -1.0)
    rank_ref[...] = rank
    ext_ref[0:ROWS, :] = hid_ref[...]
    ext_ref[ROWS:, 0:ROWS] = rank.astype(BF16)
    ext_ref[ROWS:, ROWS:] = jnp.zeros((ADAPTERS, WIDTH - ROWS), BF16)
    count = jnp.sum(chosen, axis=1, keepdims=True)
    padded = jnp.broadcast_to(jnp.floor((count + (TILE - 1)) * (1.0 / TILE)) * TILE, (ADAPTERS, 128))
    lower = jnp.where(iota((ADAPTERS, ADAPTERS), 1) < iota((ADAPTERS, ADAPTERS), 0), 1.0, 0.0)
    off_ref[...] = dot(lower.astype(BF16), padded.astype(BF16), 1, 0).astype(jnp.int32)


def plan(subsets, hidden):
    return pl.pallas_call(
        plan_kernel,
        out_shape=(
            jax.ShapeDtypeStruct((ROWS + ADAPTERS, WIDTH), BF16),
            jax.ShapeDtypeStruct((ADAPTERS, ROWS), F32),
            jax.ShapeDtypeStruct((ADAPTERS, 128), jnp.int32),
        ),
        in_specs=[whole(), whole()],
        out_specs=(whole(), whole(), whole()),
        compiler_params=params(),
        name="plan",
    )(subsets.T, hidden)


def query_kernel(hid_ref, w_ref, out_ref):
    out_ref[0] = dot(hid_ref[...], w_ref[...], 1, 0).astype(BF16)


def query_parts(hidden, weight):
    return pl.pallas_call(
        query_kernel,
        out_shape=jax.ShapeDtypeStruct((4, ROWS, WIDTH), BF16),
        grid=(4,),
        in_specs=[
            pl.BlockSpec((ROWS, WIDTH), lambda j: (0, 0)),
            pl.BlockSpec((WIDTH, WIDTH), lambda j: (0, j)),
        ],
        out_specs=pl.BlockSpec((1, ROWS, WIDTH), lambda j: (j, 0, 0)),
        compiler_params=params(),
        name="query_parts",
    )(hidden, weight)


def probe_kernel(q_ref, w_ref, hid_ref, probe_ref, own_ref, acc):
    j = pl.program_id(0)

    @pl.when(j == 0)
    def _():
        acc[...] = jnp.zeros_like(acc)

    acc[...] += dot(q_ref[0], w_ref[...], 1, 1)

    @pl.when(j == 3)
    def _():
        probe = acc[...].astype(BF16)
        probe_ref[...] = probe
        own = jnp.sum(probe.astype(F32) * hid_ref[...].astype(F32), axis=1, keepdims=True)
        own_ref[...] = jnp.broadcast_to(own, (ROWS, 128)).T[0:8, :]


def probe_of(query, weight, hidden):
    return pl.pallas_call(
        probe_kernel,
        out_shape=(
            jax.ShapeDtypeStruct((ROWS, WIDTH), BF16),
            jax.ShapeDtypeStruct((8, ROWS), F32),
        ),
        grid=(4,),
        in_specs=[
            pl.BlockSpec((1, ROWS, WIDTH), lambda j: (j, 0, 0)),
            pl.BlockSpec((WIDTH, WIDTH), lambda j: (0, j)),
            pl.BlockSpec((ROWS, WIDTH), lambda j: (0, 0)),
        ],
        out_specs=(
            pl.BlockSpec((ROWS, WIDTH), lambda j: (0, 0)),
            pl.BlockSpec((8, ROWS), lambda j: (0, 0)),
        ),
        scratch_shapes=[pltpu.VMEM((ROWS, WIDTH), F32)],
        compiler_params=params(),
        name="probe",
    )(query, weight, hidden)


def adapter_of(pos_ref, sx, sy, rc):
    y = (pos_ref[0] + (4 - sy)) & 3
    x = (pos_ref[1] + (4 - sx)) & 3
    return (y * 4 + x) * 2 + (pos_ref[2] ^ rc)


def squeeze_kernel(pos_ref, *refs):
    exts, weights, outs, rows = refs[:4], refs[4:12], refs[12:16], refs[16]
    for s in range(4):
        rows[s * ROWS : (s + 1) * ROWS, :] = exts[s][0:ROWS, :]
    ids = iota((ADAPTERS, ROWS), 0)
    slots = iota((CAP, ROWS), 0).astype(F32)
    for i in range(8):
        a = adapter_of(pos_ref, 0, i // 2, i % 2)
        part = dot(rows[...], weights[i][...], 1, 0).astype(BF16)
        for s in range(4):
            ranks = exts[s][ROWS:, 0:ROWS].astype(F32)
            mine = jnp.sum(jnp.where(ids == a, ranks, 0.0), axis=0, keepdims=True)
            pick = jnp.where(slots == mine, 1.0, 0.0).astype(BF16)
            outs[s][i] = dot(pick, part[s * ROWS : (s + 1) * ROWS, :], 1, 0).astype(BF16)


def squeeze(pos, exts, weights):
    return pl.pallas_call(
        squeeze_kernel,
        out_shape=[jax.ShapeDtypeStruct((8, CAP, B), BF16)] * 4,
        in_specs=[pl.BlockSpec(memory_space=pltpu.SMEM)] + [whole()] * 12,
        out_specs=[whole()] * 4,
        scratch_shapes=[pltpu.VMEM((4 * ROWS, WIDTH), BF16)],
        compiler_params=params(),
        name="squeeze",
    )(pos, *exts, *weights)


def pack_kernel(pos_ref, off_ref, *refs):
    blocks, outs, buf = refs[:4], refs[4:8], refs[8]
    buf[...] = jnp.zeros_like(buf)
    for t in range(4):
        for i in range(8):
            a = adapter_of(pos_ref, t, i // 2, i % 2)
            at = pl.ds(pl.multiple_of(off_ref[a], TILE), CAP)
            buf[at, :] = buf[at, :] + blocks[t][i]
    for s in range(4):
        p = (pos_ref[3] + s) & 3
        outs[s][...] = buf[pl.ds(pl.multiple_of(p * PIECE, TILE), PIECE), :]


def pack(pos, off, blocks):
    return pl.pallas_call(
        pack_kernel,
        out_shape=[jax.ShapeDtypeStruct((PIECE, B), BF16)] * 4,
        in_specs=[pl.BlockSpec(memory_space=pltpu.SMEM)] * 2 + [whole()] * 4,
        out_specs=[whole()] * 4,
        scratch_shapes=[pltpu.VMEM((BUF, B), BF16)],
        compiler_params=params(),
        name="pack",
    )(pos, off, *blocks)


def unpack_into(buf, pos_ref, pieces):
    for s in range(4):
        p = (pos_ref[3] + (4 - s)) & 3
        buf[pl.ds(pl.multiple_of(p * PIECE, TILE), PIECE), :] = pieces[s][...]
    buf[PAIRS:, :] = jnp.zeros((CAP, B), BF16)


PER = 4


def logits_kernel(pos_ref, off_ref, g0, g1, g2, g3, rank_ref, probe_ref, own_ref, up_ref, out_ref, buf):
    step = pl.program_id(0)

    @pl.when(step == 0)
    def _():
        unpack_into(buf, pos_ref, (g0, g1, g2, g3))
        out_ref[ADAPTERS:, :] = own_ref[...]

    slots = iota((CAP, ROWS), 0).astype(F32)
    for k in range(PER):
        a = step * PER + k
        seg = buf[pl.ds(pl.multiple_of(off_ref[a], TILE), CAP), :]
        pick = jnp.where(slots == rank_ref[pl.ds(a, 1), :], 1.0, 0.0).astype(BF16)
        spread = dot(seg, pick, 0, 0)
        turned = dot(up_ref[k], probe_ref[...], 1, 1)
        out_ref[pl.ds(a, 1), :] = jnp.sum(spread * turned, axis=0, keepdims=True)


def smem():
    return pl.BlockSpec(memory_space=pltpu.SMEM)


def const(shape):
    return pl.BlockSpec(shape, lambda i: (0,) * len(shape))


def logits_of(pos, off, pieces, rank, probe, own, up):
    return pl.pallas_call(
        logits_kernel,
        out_shape=jax.ShapeDtypeStruct((ADAPTERS + 8, ROWS), F32),
        grid=(ADAPTERS // PER,),
        in_specs=[smem(), smem()]
        + [const((PIECE, B))] * 4
        + [const((ADAPTERS, ROWS)), const((ROWS, WIDTH)), const((8, ROWS))]
        + [pl.BlockSpec((PER, B, WIDTH), lambda i: (i, 0, 0))],
        out_specs=const((ADAPTERS + 8, ROWS)),
        scratch_shapes=[pltpu.VMEM((BUF, B), BF16)],
        compiler_params=params(),
        name="logits",
    )(pos, off, *pieces, rank, probe, own, up)


def join_kernel(
    pos_ref, off_ref, g0, g1, g2, g3, l0, l1, l2, l3, rank_ref, hid_ref, up_ref, out_ref, buf, share, mix, acc
):
    step = pl.program_id(0)

    @pl.when(step == 0)
    def _():
        unpack_into(buf, pos_ref, (g0, g1, g2, g3))
        total = (l0[...] + l1[...]) + (l2[...] + l3[...])
        logits = (total[0:ADAPTERS] + total[ADAPTERS : ADAPTERS + 1]) * D ** (-0.5)
        chosen = rank_ref[...] >= 0.0
        logits = jnp.where(chosen, logits, -jnp.inf)
        e = jnp.where(chosen, jnp.exp(logits - jnp.max(logits, axis=0, keepdims=True)), 0.0)
        share[...] = e / jnp.sum(e, axis=0, keepdims=True)
        acc[...] = hid_ref[...].astype(F32)

    slots = iota((CAP, ROWS), 0).astype(F32)
    for k in range(PER):
        a = step * PER + k
        seg = buf[pl.ds(pl.multiple_of(off_ref[a], TILE), CAP), :]
        pick = jnp.where(slots == rank_ref[pl.ds(a, 1), :], share[pl.ds(a, 1), :], 0.0).astype(BF16)
        mix[:, k * B : (k + 1) * B] = dot(pick, seg, 0, 0).astype(BF16)
    acc[...] += dot(mix[...], up_ref[...].reshape(PER * B, WIDTH), 1, 0)

    @pl.when(step == ADAPTERS // PER - 1)
    def _():
        out_ref[...] = acc[...].astype(BF16)


def join(pos, off, pieces, parts, rank, hidden, up):
    return pl.pallas_call(
        join_kernel,
        out_shape=jax.ShapeDtypeStruct((ROWS, WIDTH), BF16),
        grid=(ADAPTERS // PER,),
        in_specs=[smem(), smem()]
        + [const((PIECE, B))] * 4
        + [const((ADAPTERS + 8, ROWS))] * 4
        + [const((ADAPTERS, ROWS)), const((ROWS, WIDTH))]
        + [pl.BlockSpec((PER, B, WIDTH), lambda i: (i, 0, 0))],
        out_specs=const((ROWS, WIDTH)),
        scratch_shapes=[
            pltpu.VMEM((BUF, B), BF16),
            pltpu.VMEM((ADAPTERS, ROWS), F32),
            pltpu.VMEM((ROWS, PER * B), BF16),
            pltpu.VMEM((ROWS, WIDTH), F32),
        ],
        compiler_params=params(),
        name="join",
    )(pos, off, *pieces, *parts, rank, hidden, up)


def shifted(x, axis, s):
    return lax.ppermute(x, axis, [(i, (i + s) % 4) for i in range(4)])


def round_trip(x, axis):
    return [x] + [shifted(x, axis, s) for s in (1, 2, 3)]


def per_device(hidden, subsets, down_weight, up_weight, query_weight, key_weight):
    pos = jnp.stack([lax.axis_index(n) for n in ("y", "x", "core", "mp")]).astype(jnp.int32)
    up = lax.all_gather(up_weight, ("y", "x", "core"), axis=0, tiled=True)
    ext, rank, off = plan(subsets, hidden)
    off = off[:, 0]

    downs = round_trip(down_weight[0], "y")
    swap = [(0, 1), (1, 0)]
    weights = []
    for w in downs:
        weights += [w, lax.ppermute(w, "core", swap)]
    exts = round_trip(ext, "x")

    parts = query_parts(hidden, query_weight)
    parts = lax.all_to_all(parts, "mp", 0, 0, tiled=True)
    query = jnp.sum(parts.astype(F32), axis=0).astype(BF16)
    query = lax.all_to_all(jnp.broadcast_to(query[None], (4, ROWS, WIDTH)), "mp", 0, 0, tiled=True)
    probe, own = probe_of(query, key_weight, hidden)

    made = squeeze(pos, exts, weights)
    back = [made[0]] + [shifted(made[4 - t], "x", t) for t in (1, 2, 3)]
    sent = pack(pos, off, back)
    got = [sent[0]] + [shifted(sent[s], "mp", s) for s in (1, 2, 3)]
    total = (got[0].astype(F32) + got[1].astype(F32)) + (got[2].astype(F32) + got[3].astype(F32))
    bottle = jnp.maximum(total, 0.0).astype(BF16)
    pieces = round_trip(bottle, "mp")

    partial = logits_of(pos, off, pieces, rank, probe, own, up)
    partials = round_trip(partial, "mp")
    return join(pos, off, pieces, partials, rank, hidden, up)


def solution(mesh):
    split = Mesh(mesh.devices.reshape(4, 4, 2, 4), ("y", "x", "core", "mp"))
    rows = ("y", "x", "core")
    return jax.shard_map(
        per_device,
        mesh=split,
        in_specs=(
            P(rows, "mp"),
            P(rows, None),
            P(rows, "mp", None),
            P(rows, None, "mp"),
            P("mp", None),
            P("mp", None),
        ),
        out_specs=P(rows, "mp"),
        check_vma=False,
    )
```

```python
import jax
import jax.numpy as jnp
from jax import lax
from jax.experimental import pallas as pl
from jax.experimental.pallas import tpu as pltpu
from jax.sharding import Mesh, PartitionSpec as P

D = 4096
ADAPTERS = 32
B = 256
CAP = 128
ROWS = 256
WIDTH = 1024
TILE = 16
PAIRS = 2560
PIECE = PAIRS // 4
BUF = PAIRS + CAP
BF16 = jnp.bfloat16
F32 = jnp.float32
VMEM = 56 * 1024 * 1024


def params(**kw):
    return pltpu.CompilerParams(vmem_limit_bytes=VMEM, **kw)


def dot(a, b, ca, cb):
    return lax.dot_general(a, b, (((ca,), (cb,)), ((), ())), preferred_element_type=F32)


def iota(shape, dim):
    return lax.broadcasted_iota(jnp.int32, shape, dim)


def whole():
    return pl.BlockSpec(memory_space=pltpu.VMEM)


def smem():
    return pl.BlockSpec(memory_space=pltpu.SMEM)


def anywhere():
    return pl.BlockSpec(memory_space=pl.ANY)


def plan_kernel(sub_ref, hid_ref, ext_ref, rank_ref, off_ref):
    ids = iota((ADAPTERS, ROWS), 0)
    chosen = jnp.zeros((ADAPTERS, ROWS), F32)
    for k in range(sub_ref.shape[0]):
        chosen = chosen + jnp.where(sub_ref[k : k + 1, :] == ids, 1.0, 0.0)
    named = chosen.astype(BF16)
    earlier = jnp.where(iota((ROWS, ROWS), 0) < iota((ROWS, ROWS), 1), 1.0, 0.0)
    before = dot(named, earlier.astype(BF16), 1, 0)
    rank = jnp.where(chosen > 0.5, before, -1.0)
    rank_ref[...] = rank
    ext_ref[0:ROWS, :] = hid_ref[...]
    ext_ref[ROWS:, 0:ROWS] = rank.astype(BF16)
    ext_ref[ROWS:, ROWS:] = jnp.zeros((ADAPTERS, WIDTH - ROWS), BF16)
    count = jnp.sum(chosen, axis=1, keepdims=True)
    padded = jnp.broadcast_to(jnp.floor((count + (TILE - 1)) * (1.0 / TILE)) * TILE, (ADAPTERS, 128))
    lower = jnp.where(iota((ADAPTERS, ADAPTERS), 1) < iota((ADAPTERS, ADAPTERS), 0), 1.0, 0.0)
    off_ref[...] = dot(lower.astype(BF16), padded.astype(BF16), 1, 0).astype(jnp.int32)


def plan(subsets, hidden):
    return pl.pallas_call(
        plan_kernel,
        out_shape=(
            jax.ShapeDtypeStruct((ROWS + ADAPTERS, WIDTH), BF16),
            jax.ShapeDtypeStruct((ADAPTERS, ROWS), F32),
            jax.ShapeDtypeStruct((ADAPTERS, 128), jnp.int32),
        ),
        in_specs=[whole(), whole()],
        out_specs=(whole(), whole(), whole()),
        compiler_params=params(),
        name="plan",
    )(subsets.T, hidden)


def spread_kernel(rank_ref, pick_ref):
    rest = jnp.full((CAP - ADAPTERS, ROWS), -1.0, F32)
    cols = jnp.concatenate([rank_ref[...], rest], axis=0).T.astype(BF16)
    slots = iota((ROWS, CAP), 1).astype(F32)
    for a in range(ADAPTERS):
        one = jnp.where(iota((CAP, CAP), 0) == a, 1.0, 0.0).astype(BF16)
        pick_ref[:, a * CAP : (a + 1) * CAP] = jnp.where(dot(cols, one, 1, 0) == slots, 1.0, 0.0).astype(BF16)


def spread(rank):
    return pl.pallas_call(
        spread_kernel,
        out_shape=jax.ShapeDtypeStruct((ROWS, ADAPTERS * CAP), BF16),
        in_specs=[whole()],
        out_specs=whole(),
        compiler_params=params(),
        name="spread",
    )(rank)


def block_copies(pos_ref, weight_ref, held, sems, sign):
    copies = []
    for s in range(4):
        p = (pos_ref[3] + (s if sign > 0 else 4 - s)) & 3
        cols = pl.ds(pl.multiple_of(p * WIDTH, WIDTH), WIDTH)
        copies.append(pltpu.make_async_copy(weight_ref.at[:, cols], held.at[s], sems.at[s]))
    for s in (2, 1, 3, 0):
        copies[s].start()
    return copies


def query_kernel(pos_ref, ext_ref, weight_ref, *refs):
    outs, held, sems = refs[:4], refs[4], refs[5]
    copies = block_copies(pos_ref, weight_ref, held, sems, 1)
    for s in (2, 1, 3, 0):
        copies[s].wait()
        outs[s][...] = dot(ext_ref[0:ROWS, :], held[s], 1, 0).astype(BF16)


def query_parts(pos, ext, weight):
    return pl.pallas_call(
        query_kernel,
        out_shape=[jax.ShapeDtypeStruct((ROWS, WIDTH), BF16)] * 4,
        in_specs=[smem(), whole(), anywhere()],
        out_specs=[whole()] * 4,
        scratch_shapes=[pltpu.VMEM((4, WIDTH, WIDTH), BF16), pltpu.SemaphoreType.DMA((4,))],
        compiler_params=params(),
        name="query_parts",
    )(pos, ext, weight)


def probe_kernel(pos_ref, q0, q1, q2, q3, hid_ref, weight_ref, probe_ref, own_ref, held, sems):
    copies = block_copies(pos_ref, weight_ref, held, sems, -1)
    total = jnp.zeros((ROWS, WIDTH), F32)
    for s, q in ((2, q2), (1, q1), (3, q3), (0, q0)):
        copies[s].wait()
        total = total + dot(q[...], held[s], 1, 1)
    probe = total.astype(BF16)
    probe_ref[...] = probe
    own = jnp.sum(probe.astype(F32) * hid_ref[...].astype(F32), axis=1, keepdims=True)
    own_ref[...] = jnp.broadcast_to(own, (ROWS, 128)).T[0:8, :]


def probe_of(pos, query, weight, hidden):
    return pl.pallas_call(
        probe_kernel,
        out_shape=(
            jax.ShapeDtypeStruct((ROWS, WIDTH), BF16),
            jax.ShapeDtypeStruct((8, ROWS), F32),
        ),
        in_specs=[smem()] + [whole()] * 5 + [anywhere()],
        out_specs=(whole(), whole()),
        scratch_shapes=[pltpu.VMEM((4, WIDTH, WIDTH), BF16), pltpu.SemaphoreType.DMA((4,))],
        compiler_params=params(),
        name="probe",
    )(pos, *query, hidden, weight)


def adapter_of(pos_ref, sx, i):
    return (i // 2 * 4 + ((pos_ref[1] + (4 - sx)) & 3)) * 2 + i % 2


def squeeze_kernel(pos_ref, *refs):
    exts, weights, outs = refs[:4], refs[4], refs[5:9]
    rows, ranks, held, row_sems, rank_sems, sems = refs[9:]
    row_copies, rank_copies = [], []
    for s in range(4):
        some = pl.ds(s * ROWS, ROWS)
        row_copies.append(pltpu.make_async_copy(exts[s].at[pl.ds(0, ROWS)], rows.at[some], row_sems.at[s]))
        rest = exts[s].at[pl.ds(ROWS, ADAPTERS), pl.ds(0, ROWS)]
        rank_copies.append(pltpu.make_async_copy(rest, ranks.at[s], rank_sems.at[s]))
    copies = [
        pltpu.make_async_copy(weights.at[i], held.at[:, pl.ds(i * B, B)], sems.at[i]) for i in range(8)
    ]
    for copy in row_copies + copies[:4] + rank_copies + copies[4:]:
        copy.start()
    ids = iota((ADAPTERS, ROWS), 0)
    slots = iota((CAP, ROWS), 0).astype(F32)
    for copy in row_copies:
        copy.wait()
    for j in range(2):
        for i in range(4 * j, 4 * j + 4):
            copies[i].wait()
        part = dot(rows[...], held[:, 4 * j * B : 4 * (j + 1) * B], 1, 0).astype(BF16)
        if j == 0:
            for copy in rank_copies:
                copy.wait()
        for i in range(4 * j, 4 * j + 4):
            a = adapter_of(pos_ref, 0, i)
            cols = slice((i - 4 * j) * B, (i - 4 * j + 1) * B)
            for s in range(4):
                mine = jnp.sum(jnp.where(ids == a, ranks[s].astype(F32), 0.0), axis=0, keepdims=True)
                pick = jnp.where(slots == mine, 1.0, 0.0).astype(BF16)
                outs[s][i] = dot(pick, part[s * ROWS : (s + 1) * ROWS, cols], 1, 0).astype(BF16)


def squeeze(pos, exts, weights):
    return pl.pallas_call(
        squeeze_kernel,
        out_shape=[jax.ShapeDtypeStruct((8, CAP, B), BF16)] * 4,
        in_specs=[smem()] + [anywhere()] * 5,
        out_specs=[whole()] * 4,
        scratch_shapes=[
            pltpu.VMEM((4 * ROWS, WIDTH), BF16),
            pltpu.VMEM((4, ADAPTERS, ROWS), BF16),
            pltpu.VMEM((WIDTH, 8 * B), BF16),
            pltpu.SemaphoreType.DMA((4,)),
            pltpu.SemaphoreType.DMA((4,)),
            pltpu.SemaphoreType.DMA((8,)),
        ],
        compiler_params=params(),
        name="squeeze",
    )(pos, *exts, weights)


def pack_kernel(pos_ref, off_ref, *refs):
    blocks, outs, buf = refs[:4], refs[4:8], refs[8]
    buf[...] = jnp.zeros_like(buf)
    for t in range(4):
        for i in range(8):
            a = adapter_of(pos_ref, t, i)
            at = pl.ds(pl.multiple_of(off_ref[a], TILE), CAP)
            buf[at, :] = buf[at, :] + blocks[t][i]
    for s in range(4):
        p = (pos_ref[3] + s) & 3
        outs[s][...] = buf[pl.ds(pl.multiple_of(p * PIECE, TILE), PIECE), :]


def pack(pos, off, blocks):
    return pl.pallas_call(
        pack_kernel,
        out_shape=[jax.ShapeDtypeStruct((PIECE, B), BF16)] * 4,
        in_specs=[pl.BlockSpec(memory_space=pltpu.SMEM)] * 2 + [whole()] * 4,
        out_specs=[whole()] * 4,
        scratch_shapes=[pltpu.VMEM((BUF, B), BF16)],
        compiler_params=params(),
        name="pack",
    )(pos, off, *blocks)


def unpack_into(buf, pos_ref, pieces):
    for s in range(4):
        p = (pos_ref[3] + (4 - s)) & 3
        buf[pl.ds(pl.multiple_of(p * PIECE, TILE), PIECE), :] = pieces[s][...]
    buf[PAIRS:, :] = jnp.zeros((CAP, B), BF16)


PER = 4
STEPS = ADAPTERS // PER
ORDER = list(range(ADAPTERS))


def step_copies(up_ref, held, bottle_ref, bottles, sems):
    copies = []
    for g in range(STEPS):
        some = pl.ds(g * PER, PER)
        cols = pl.ds(g * PER * B, PER * B)
        copies.append(
            (
                pltpu.make_async_copy(bottle_ref.at[:, cols], bottles.at[:, cols], sems.at[0, g]),
                pltpu.make_async_copy(up_ref.at[some], held.at[some], sems.at[1, g]),
            )
        )
        for copy in copies[g]:
            copy.start()

    def arrive(g):
        for copy in copies[g]:
            copy.wait()

    return arrive


def segment(buf, off_ref, a):
    return buf[pl.ds(pl.multiple_of(off_ref[a], TILE), CAP), :]


def expand_kernel(pos_ref, off_ref, g0, g1, g2, g3, pick_ref, out_ref, buf):
    unpack_into(buf, pos_ref, (g0, g1, g2, g3))
    for i, a in enumerate(ORDER):
        pick = pick_ref[:, a * CAP : (a + 1) * CAP]
        out_ref[:, i * B : (i + 1) * B] = dot(pick, segment(buf, off_ref, a), 1, 0).astype(BF16)


def expand(pos, off, pieces, pick):
    return pl.pallas_call(
        expand_kernel,
        out_shape=jax.ShapeDtypeStruct((ROWS, ADAPTERS * B), BF16),
        in_specs=[smem(), smem()] + [whole()] * 5,
        out_specs=whole(),
        scratch_shapes=[pltpu.VMEM((BUF, B), BF16)],
        compiler_params=params(),
        name="expand",
    )(pos, off, *pieces, pick)


def logits_kernel(bottle_ref, probe_ref, own_ref, up_ref, out_ref, held, bottles, sems):
    arrive = step_copies(up_ref, held, bottle_ref, bottles, sems)
    out_ref[ADAPTERS:, :] = own_ref[...]
    lane = iota((ROWS, 128), 1)
    found = jnp.zeros((ROWS, 128), F32)
    for g in range(STEPS):
        arrive(g)
        turned = dot(probe_ref[...], held[g * PER : (g + 1) * PER].reshape(PER * B, WIDTH), 1, 1)
        product = turned * bottles[:, g * PER * B : (g + 1) * PER * B].astype(F32)
        for k in range(PER):
            logit = jnp.sum(product[:, k * B : (k + 1) * B], axis=1, keepdims=True)
            found = jnp.where(lane == ORDER[g * PER + k], logit, found)
    out_ref[0:ADAPTERS, :] = found.T[0:ADAPTERS, :]


def logits_of(bottle, probe, own, up):
    return pl.pallas_call(
        logits_kernel,
        out_shape=jax.ShapeDtypeStruct((ADAPTERS + 8, ROWS), F32),
        in_specs=[anywhere()] + [whole()] * 2 + [anywhere()],
        out_specs=whole(),
        scratch_shapes=[
            pltpu.VMEM((ADAPTERS, B, WIDTH), BF16),
            pltpu.VMEM((ROWS, ADAPTERS * B), BF16),
            pltpu.SemaphoreType.DMA((2, STEPS)),
        ],
        compiler_params=params(),
        name="logits",
    )(bottle, probe, own, up)


def join_kernel(bottle_ref, l0, l1, l2, l3, rank_ref, hid_ref, up_ref, out_ref, held, bottles, sems):
    arrive = step_copies(up_ref, held, bottle_ref, bottles, sems)
    total = (l0[...] + l1[...]) + (l2[...] + l3[...])
    logits = (total[0:ADAPTERS] + total[ADAPTERS : ADAPTERS + 1]) * D ** (-0.5)
    chosen = rank_ref[...] >= 0.0
    logits = jnp.where(chosen, logits, -jnp.inf)
    e = jnp.where(chosen, jnp.exp(logits - jnp.max(logits, axis=0, keepdims=True)), 0.0)
    share = e / jnp.sum(e, axis=0, keepdims=True)
    share = jnp.concatenate([share, jnp.zeros((128 - ADAPTERS, ROWS), F32)], axis=0).T
    total = hid_ref[...].astype(F32)
    for g in range(STEPS):
        mix = []
        arrive(g)
        for i in range(g * PER, (g + 1) * PER):
            a = ORDER[i]
            bottle = bottles[:, i * B : (i + 1) * B].astype(F32)
            mix.append((bottle * share[:, a : a + 1]).astype(BF16))
        up = held[g * PER : (g + 1) * PER].reshape(PER * B, WIDTH)
        total = total + dot(jnp.concatenate(mix, axis=1), up, 1, 0)
    out_ref[...] = total.astype(BF16)


def join(bottle, parts, rank, hidden, up):
    return pl.pallas_call(
        join_kernel,
        out_shape=jax.ShapeDtypeStruct((ROWS, WIDTH), BF16),
        in_specs=[anywhere()] + [whole()] * 6 + [anywhere()],
        out_specs=whole(),
        scratch_shapes=[
            pltpu.VMEM((ADAPTERS, B, WIDTH), BF16),
            pltpu.VMEM((ROWS, ADAPTERS * B), BF16),
            pltpu.SemaphoreType.DMA((2, STEPS)),
        ],
        compiler_params=params(),
        name="join",
    )(bottle, *parts, rank, hidden, up)


def shifted(x, axis, s):
    return lax.ppermute(x, axis, [(i, (i + s) % 4) for i in range(4)])


def round_trip(x, axis):
    return [x] + [shifted(x, axis, s) for s in (1, 2, 3)]


def gathered(xs, axis):
    return [xs[0]] + [shifted(xs[s], axis, s) for s in (1, 2, 3)]


def summed(xs):
    xs = [x.astype(F32) for x in xs]
    return (xs[0] + xs[1]) + (xs[2] + xs[3])


def per_device(hidden, subsets, down_weight, up_weight, query_weight, key_weight):
    pos = jnp.stack([lax.axis_index(n) for n in ("y", "x", "core", "mp")]).astype(jnp.int32)
    ext, rank, off = plan(subsets, hidden)
    pick = spread(rank)
    off = off[:, 0]

    parts = query_parts(pos, ext, query_weight)
    downs = lax.all_gather(down_weight, ("y", "core"), axis=0, tiled=True)
    exts = round_trip(ext, "x")
    near = [parts[0]] + [shifted(parts[s], "mp", s) for s in (1, 3)]
    phase = (exts, downs, near, parts[2], pick, up_weight)
    exts, downs, near, far, pick, up_weight = lax.optimization_barrier(phase)
    parts = near + [shifted(far, "mp", 2)]

    up = lax.all_gather(up_weight, ("y", "x", "core"), axis=0, tiled=True)
    made = squeeze(pos, exts, downs)
    back = gathered([made[0], made[3], made[2], made[1]], "x")
    query = summed(parts).astype(BF16)
    query = round_trip(query, "mp")

    sent = pack(pos, off, back)
    probe, own = probe_of(pos, query, key_weight, hidden)
    got = gathered(sent, "mp")
    got, probe = lax.optimization_barrier((got, probe))
    pieces = round_trip(jnp.maximum(summed(got), 0.0).astype(BF16), "mp")

    bottle = expand(pos, off, pieces, pick)
    partial = logits_of(bottle, probe, own, up)
    partials = round_trip(partial, "mp")
    return join(bottle, partials, rank, hidden, up)


def solution(mesh):
    split = Mesh(mesh.devices.reshape(4, 4, 2, 4), ("y", "x", "core", "mp"))
    rows = ("y", "x", "core")
    return jax.shard_map(
        per_device,
        mesh=split,
        in_specs=(
            P(rows, "mp"),
            P(rows, None),
            P(rows, "mp", None),
            P(rows, None, "mp"),
            P("mp", None),
            P("mp", None),
        ),
        out_specs=P(rows, "mp"),
        check_vma=False,
    )
```

```python
import jax
import jax.numpy as jnp
from jax import lax
from jax.experimental import pallas as pl
from jax.experimental.pallas import tpu as pltpu
from jax.sharding import Mesh, PartitionSpec as P

D = 4096
ADAPTERS = 32
B = 256
CAP = 128
ROWS = 256
WIDTH = 1024
TILE = 16
PAIRS = 2560
PIECE = PAIRS // 4
BUF = PAIRS + CAP
BF16 = jnp.bfloat16
F32 = jnp.float32
VMEM = 56 * 1024 * 1024


def params(limit=VMEM):
    return pltpu.CompilerParams(vmem_limit_bytes=limit)


def dot(a, b, ca, cb):
    return lax.dot_general(a, b, (((ca,), (cb,)), ((), ())), preferred_element_type=F32)


def iota(shape, dim):
    return lax.broadcasted_iota(jnp.int32, shape, dim)


def whole():
    return pl.BlockSpec(memory_space=pltpu.VMEM)


def smem():
    return pl.BlockSpec(memory_space=pltpu.SMEM)


def anywhere():
    return pl.BlockSpec(memory_space=pl.ANY)


def plan_kernel(sub_ref, hid_ref, ext_ref, rank_ref, off_ref):
    ids = iota((ADAPTERS, ROWS), 0)
    chosen = jnp.zeros((ADAPTERS, ROWS), F32)
    for k in range(sub_ref.shape[0]):
        chosen = chosen + jnp.where(sub_ref[k : k + 1, :] == ids, 1.0, 0.0)
    named = chosen.astype(BF16)
    earlier = jnp.where(iota((ROWS, ROWS), 0) < iota((ROWS, ROWS), 1), 1.0, 0.0)
    before = dot(named, earlier.astype(BF16), 1, 0)
    rank = jnp.where(chosen > 0.5, before, -1.0)
    rank_ref[...] = rank
    ext_ref[0:ROWS, :] = hid_ref[...]
    ext_ref[ROWS:, 0:ROWS] = rank.astype(BF16)
    ext_ref[ROWS:, ROWS:] = jnp.zeros((ADAPTERS, WIDTH - ROWS), BF16)
    count = jnp.sum(chosen, axis=1, keepdims=True)
    padded = jnp.broadcast_to(jnp.floor((count + (TILE - 1)) * (1.0 / TILE)) * TILE, (ADAPTERS, 128))
    lower = jnp.where(iota((ADAPTERS, ADAPTERS), 1) < iota((ADAPTERS, ADAPTERS), 0), 1.0, 0.0)
    off_ref[...] = dot(lower.astype(BF16), padded.astype(BF16), 1, 0).astype(jnp.int32)


def plan(subsets, hidden):
    return pl.pallas_call(
        plan_kernel,
        out_shape=(
            jax.ShapeDtypeStruct((ROWS + ADAPTERS, WIDTH), BF16),
            jax.ShapeDtypeStruct((ADAPTERS, ROWS), F32),
            jax.ShapeDtypeStruct((ADAPTERS, 128), jnp.int32),
        ),
        in_specs=[whole(), whole()],
        out_specs=(whole(), whole(), whole()),
        compiler_params=params(),
        name="plan",
    )(subsets.T, hidden)


def spread_kernel(rank_ref, pick_ref):
    rest = jnp.full((CAP - ADAPTERS, ROWS), -1.0, F32)
    cols = jnp.concatenate([rank_ref[...], rest], axis=0).T.astype(BF16)
    slots = iota((ROWS, CAP), 1).astype(F32)
    for a in range(ADAPTERS):
        one = jnp.where(iota((CAP, CAP), 0) == a, 1.0, 0.0).astype(BF16)
        pick_ref[:, a * CAP : (a + 1) * CAP] = jnp.where(dot(cols, one, 1, 0) == slots, 1.0, 0.0).astype(BF16)


def spread(rank):
    return pl.pallas_call(
        spread_kernel,
        out_shape=jax.ShapeDtypeStruct((ROWS, ADAPTERS * CAP), BF16),
        in_specs=[whole()],
        out_specs=whole(),
        compiler_params=params(),
        name="spread",
    )(rank)


def block_copies(pos_ref, weight_ref, held, sems, sign):
    copies = []
    for s in range(4):
        p = (pos_ref[3] + (s if sign > 0 else 4 - s)) & 3
        cols = pl.ds(pl.multiple_of(p * WIDTH, WIDTH), WIDTH)
        copies.append(pltpu.make_async_copy(weight_ref.at[:, cols], held.at[s], sems.at[s]))
    for s in (2, 1, 3, 0):
        copies[s].start()
    return copies


def query_kernel(pos_ref, ext_ref, weight_ref, *refs):
    outs, held, sems = refs[:4], refs[4], refs[5]
    copies = block_copies(pos_ref, weight_ref, held, sems, 1)
    for s in (2, 1, 3, 0):
        copies[s].wait()
        outs[s][...] = dot(ext_ref[0:ROWS, :], held[s], 1, 0).astype(BF16)


def query_parts(pos, ext, weight):
    return pl.pallas_call(
        query_kernel,
        out_shape=[jax.ShapeDtypeStruct((ROWS, WIDTH), BF16)] * 4,
        in_specs=[smem(), whole(), anywhere()],
        out_specs=[whole()] * 4,
        scratch_shapes=[pltpu.VMEM((4, WIDTH, WIDTH), BF16), pltpu.SemaphoreType.DMA((4,))],
        compiler_params=params(),
        name="query_parts",
    )(pos, ext, weight)


def probe_kernel(pos_ref, q0, q1, q2, q3, hid_ref, weight_ref, probe_ref, own_ref, held, sems):
    copies = block_copies(pos_ref, weight_ref, held, sems, -1)
    total = jnp.zeros((ROWS, WIDTH), F32)
    for s, q in ((2, q2), (1, q1), (3, q3), (0, q0)):
        copies[s].wait()
        total = total + dot(q[...], held[s], 1, 1)
    probe = total.astype(BF16)
    probe_ref[...] = probe
    own = jnp.sum(probe.astype(F32) * hid_ref[...].astype(F32), axis=1, keepdims=True)
    own_ref[...] = jnp.broadcast_to(own, (ROWS, 128)).T[0:8, :]


def probe_of(pos, query, weight, hidden):
    return pl.pallas_call(
        probe_kernel,
        out_shape=(
            jax.ShapeDtypeStruct((ROWS, WIDTH), BF16),
            jax.ShapeDtypeStruct((8, ROWS), F32),
        ),
        in_specs=[smem()] + [whole()] * 5 + [anywhere()],
        out_specs=(whole(), whole()),
        scratch_shapes=[pltpu.VMEM((4, WIDTH, WIDTH), BF16), pltpu.SemaphoreType.DMA((4,))],
        compiler_params=params(),
        name="probe",
    )(pos, *query, hidden, weight)


def adapter_of(pos_ref, sx, i):
    return (i // 2 * 4 + ((pos_ref[1] + (4 - sx)) & 3)) * 2 + i % 2


def squeeze_kernel(pos_ref, *refs):
    exts, weights, outs = refs[:4], refs[4], refs[5:9]
    rows, ranks, held, row_sems, rank_sems, sems = refs[9:]
    row_copies, rank_copies = [], []
    for s in range(4):
        some = pl.ds(s * ROWS, ROWS)
        row_copies.append(pltpu.make_async_copy(exts[s].at[pl.ds(0, ROWS)], rows.at[some], row_sems.at[s]))
        rest = exts[s].at[pl.ds(ROWS, ADAPTERS), pl.ds(0, ROWS)]
        rank_copies.append(pltpu.make_async_copy(rest, ranks.at[s], rank_sems.at[s]))
    copies = [
        pltpu.make_async_copy(weights.at[i], held.at[:, pl.ds(i * B, B)], sems.at[i]) for i in range(8)
    ]
    for copy in row_copies + copies[:4] + rank_copies + copies[4:]:
        copy.start()
    ids = iota((ADAPTERS, ROWS), 0)
    slots = iota((CAP, ROWS), 0).astype(F32)
    for copy in row_copies:
        copy.wait()
    for j in range(2):
        for i in range(4 * j, 4 * j + 4):
            copies[i].wait()
        part = dot(rows[...], held[:, 4 * j * B : 4 * (j + 1) * B], 1, 0).astype(BF16)
        if j == 0:
            for copy in rank_copies:
                copy.wait()
        for i in range(4 * j, 4 * j + 4):
            a = adapter_of(pos_ref, 0, i)
            cols = slice((i - 4 * j) * B, (i - 4 * j + 1) * B)
            for s in range(4):
                mine = jnp.sum(jnp.where(ids == a, ranks[s].astype(F32), 0.0), axis=0, keepdims=True)
                pick = jnp.where(slots == mine, 1.0, 0.0).astype(BF16)
                outs[s][i] = dot(pick, part[s * ROWS : (s + 1) * ROWS, cols], 1, 0).astype(BF16)


def squeeze(pos, exts, weights):
    return pl.pallas_call(
        squeeze_kernel,
        out_shape=[jax.ShapeDtypeStruct((8, CAP, B), BF16)] * 4,
        in_specs=[smem()] + [anywhere()] * 5,
        out_specs=[whole()] * 4,
        scratch_shapes=[
            pltpu.VMEM((4 * ROWS, WIDTH), BF16),
            pltpu.VMEM((4, ADAPTERS, ROWS), BF16),
            pltpu.VMEM((WIDTH, 8 * B), BF16),
            pltpu.SemaphoreType.DMA((4,)),
            pltpu.SemaphoreType.DMA((4,)),
            pltpu.SemaphoreType.DMA((8,)),
        ],
        compiler_params=params(),
        name="squeeze",
    )(pos, *exts, weights)


def pack_kernel(pos_ref, off_ref, *refs):
    blocks, outs, buf = refs[:4], refs[4:8], refs[8]
    buf[...] = jnp.zeros_like(buf)
    for t in range(4):
        for i in range(8):
            a = adapter_of(pos_ref, t, i)
            at = pl.ds(pl.multiple_of(off_ref[a], TILE), CAP)
            buf[at, :] = buf[at, :] + blocks[t][i]
    for s in range(4):
        p = (pos_ref[3] + s) & 3
        outs[s][...] = buf[pl.ds(pl.multiple_of(p * PIECE, TILE), PIECE), :]


def pack(pos, off, blocks):
    return pl.pallas_call(
        pack_kernel,
        out_shape=[jax.ShapeDtypeStruct((PIECE, B), BF16)] * 4,
        in_specs=[pl.BlockSpec(memory_space=pltpu.SMEM)] * 2 + [whole()] * 4,
        out_specs=[whole()] * 4,
        scratch_shapes=[pltpu.VMEM((BUF, B), BF16)],
        compiler_params=params(),
        name="pack",
    )(pos, off, *blocks)


def unpack_into(buf, pos_ref, pieces):
    for s in range(4):
        p = (pos_ref[3] + (4 - s)) & 3
        buf[pl.ds(pl.multiple_of(p * PIECE, TILE), PIECE), :] = pieces[s][...]
    buf[PAIRS:, :] = jnp.zeros((CAP, B), BF16)


PER = 4
STEPS = ADAPTERS // PER
ORDER = list(range(ADAPTERS))


def step_copies(up_ref, held, bottle_ref, bottles, sems):
    copies = []
    for g in range(STEPS):
        some = pl.ds(g * PER, PER)
        cols = pl.ds(g * PER * B, PER * B)
        copies.append(
            (
                pltpu.make_async_copy(bottle_ref.at[:, cols], bottles.at[:, cols], sems.at[0, g]),
                pltpu.make_async_copy(up_ref.at[some], held.at[some], sems.at[1, g]),
            )
        )
        for copy in copies[g]:
            copy.start()

    def arrive(g):
        for copy in copies[g]:
            copy.wait()

    return arrive


def segment(buf, off_ref, a):
    return buf[pl.ds(pl.multiple_of(off_ref[a], TILE), CAP), :]


def expand_kernel(pos_ref, off_ref, g0, g1, g2, g3, pick_ref, out_ref, buf):
    unpack_into(buf, pos_ref, (g0, g1, g2, g3))
    for i, a in enumerate(ORDER):
        pick = pick_ref[:, a * CAP : (a + 1) * CAP]
        out_ref[:, i * B : (i + 1) * B] = dot(pick, segment(buf, off_ref, a), 1, 0).astype(BF16)


def expand(pos, off, pieces, pick):
    return pl.pallas_call(
        expand_kernel,
        out_shape=jax.ShapeDtypeStruct((ROWS, ADAPTERS * B), BF16),
        in_specs=[smem(), smem()] + [whole()] * 5,
        out_specs=whole(),
        scratch_shapes=[pltpu.VMEM((BUF, B), BF16)],
        compiler_params=params(),
        name="expand",
    )(pos, off, *pieces, pick)


def logits_kernel(bottle_ref, probe_ref, own_ref, up_ref, out_ref, held, bottles, sems):
    arrive = step_copies(up_ref, held, bottle_ref, bottles, sems)
    out_ref[ADAPTERS:, :] = own_ref[...]
    lane = iota((ROWS, 128), 1)
    found = jnp.zeros((ROWS, 128), F32)
    turned = None
    for g in range(STEPS + 1):
        before = turned
        if g < STEPS:
            arrive(g)
            turned = dot(probe_ref[...], held[g * PER : (g + 1) * PER].reshape(PER * B, WIDTH), 1, 1)
        for i in range((g - 1) * PER, g * PER) if g else ():
            k = i % PER
            bottle = bottles[:, i * B : (i + 1) * B].astype(F32)
            logit = jnp.sum(before[:, k * B : (k + 1) * B] * bottle, axis=1, keepdims=True)
            found = jnp.where(lane == ORDER[i], logit, found)
    out_ref[0:ADAPTERS, :] = found.T[0:ADAPTERS, :]


LESS = 48 * 1024 * 1024


def logits_of(bottle, probe, own, up):
    return pl.pallas_call(
        logits_kernel,
        out_shape=jax.ShapeDtypeStruct((ADAPTERS + 8, ROWS), F32),
        in_specs=[anywhere()] + [whole()] * 2 + [anywhere()],
        out_specs=whole(),
        scratch_shapes=[
            pltpu.VMEM((ADAPTERS, B, WIDTH), BF16),
            pltpu.VMEM((ROWS, ADAPTERS * B), BF16),
            pltpu.SemaphoreType.DMA((2, STEPS)),
        ],
        compiler_params=params(),
        name="logits",
    )(bottle, probe, own, up)


def join_kernel(bottles, l0, l1, l2, l3, rank_ref, hid_ref, up_ref, out_ref, held, sems):
    copies = []
    for g in range(STEPS):
        some = pl.ds(g * PER, PER)
        copies.append(pltpu.make_async_copy(up_ref.at[some], held.at[some], sems.at[g]))
        copies[g].start()
    total = (l0[...] + l1[...]) + (l2[...] + l3[...])
    logits = (total[0:ADAPTERS] + total[ADAPTERS : ADAPTERS + 1]) * D ** (-0.5)
    chosen = rank_ref[...] >= 0.0
    logits = jnp.where(chosen, logits, -jnp.inf)
    e = jnp.where(chosen, jnp.exp(logits - jnp.max(logits, axis=0, keepdims=True)), 0.0)
    share = e / jnp.sum(e, axis=0, keepdims=True)
    share = jnp.concatenate([share, jnp.zeros((128 - ADAPTERS, ROWS), F32)], axis=0).T
    total = hid_ref[...].astype(F32)
    for g in range(STEPS):
        mix = []
        for i in range(g * PER, (g + 1) * PER):
            a = ORDER[i]
            bottle = bottles[:, i * B : (i + 1) * B].astype(F32)
            mix.append((bottle * share[:, a : a + 1]).astype(BF16))
        copies[g].wait()
        up = held[g * PER : (g + 1) * PER].reshape(PER * B, WIDTH)
        total = total + dot(jnp.concatenate(mix, axis=1), up, 1, 0)
    out_ref[...] = total.astype(BF16)


def join(bottle, parts, rank, hidden, up):
    return pl.pallas_call(
        join_kernel,
        out_shape=jax.ShapeDtypeStruct((ROWS, WIDTH), BF16),
        in_specs=[whole()] * 7 + [anywhere()],
        out_specs=whole(),
        scratch_shapes=[
            pltpu.VMEM((ADAPTERS, B, WIDTH), BF16),
            pltpu.SemaphoreType.DMA((STEPS,)),
        ],
        compiler_params=params(LESS),
        name="join",
    )(bottle, *parts, rank, hidden, up)


def shifted(x, axis, s):
    return lax.ppermute(x, axis, [(i, (i + s) % 4) for i in range(4)])


def round_trip(x, axis):
    return [x] + [shifted(x, axis, s) for s in (1, 2, 3)]


def gathered(xs, axis):
    return [xs[0]] + [shifted(xs[s], axis, s) for s in (1, 2, 3)]


def summed(xs):
    xs = [x.astype(F32) for x in xs]
    return (xs[0] + xs[1]) + (xs[2] + xs[3])


def per_device(hidden, subsets, down_weight, up_weight, query_weight, key_weight):
    pos = jnp.stack([lax.axis_index(n) for n in ("y", "x", "core", "mp")]).astype(jnp.int32)
    ext, rank, off = plan(subsets, hidden)
    pick = spread(rank)
    off = off[:, 0]

    parts = query_parts(pos, ext, query_weight)
    downs = lax.all_gather(down_weight, ("y", "core"), axis=0, tiled=True)
    exts = round_trip(ext, "x")
    near = [parts[0]] + [shifted(parts[s], "mp", s) for s in (1, 3)]
    phase = (exts, downs, near, parts[2], pick, up_weight)
    exts, downs, near, far, pick, up_weight = lax.optimization_barrier(phase)
    parts = near + [shifted(far, "mp", 2)]

    up = lax.all_gather(up_weight, ("y", "x", "core"), axis=0, tiled=True)
    made = squeeze(pos, exts, downs)
    back = gathered([made[0], made[3], made[2], made[1]], "x")
    query = summed(parts).astype(BF16)
    query = round_trip(query, "mp")

    sent = pack(pos, off, back)
    probe, own = probe_of(pos, query, key_weight, hidden)
    got = gathered(sent, "mp")
    got, probe = lax.optimization_barrier((got, probe))
    pieces = round_trip(jnp.maximum(summed(got), 0.0).astype(BF16), "mp")

    bottle = expand(pos, off, pieces, pick)
    partial = logits_of(bottle, probe, own, up)
    partials = round_trip(partial, "mp")
    return join(bottle, partials, rank, hidden, up)


def solution(mesh):
    split = Mesh(mesh.devices.reshape(4, 4, 2, 4), ("y", "x", "core", "mp"))
    rows = ("y", "x", "core")
    return jax.shard_map(
        per_device,
        mesh=split,
        in_specs=(
            P(rows, "mp"),
            P(rows, None),
            P(rows, "mp", None),
            P(rows, None, "mp"),
            P("mp", None),
            P("mp", None),
        ),
        out_specs=P(rows, "mp"),
        check_vma=False,
    )
```

```python
import jax
import jax.numpy as jnp
from jax import lax
from jax.experimental import pallas as pl
from jax.experimental.pallas import tpu as pltpu
from jax.sharding import Mesh, PartitionSpec as P

D = 4096
ADAPTERS = 32
B = 256
CAP = 128
ROWS = 256
WIDTH = 1024
TILE = 16
PAIRS = 2560
PIECE = PAIRS // 4
BUF = PAIRS + CAP
BF16 = jnp.bfloat16
F32 = jnp.float32
VMEM = 56 * 1024 * 1024


def params(limit=VMEM):
    return pltpu.CompilerParams(vmem_limit_bytes=limit)


def dot(a, b, ca, cb):
    return lax.dot_general(a, b, (((ca,), (cb,)), ((), ())), preferred_element_type=F32)


def iota(shape, dim):
    return lax.broadcasted_iota(jnp.int32, shape, dim)


def whole():
    return pl.BlockSpec(memory_space=pltpu.VMEM)


def smem():
    return pl.BlockSpec(memory_space=pltpu.SMEM)


def anywhere():
    return pl.BlockSpec(memory_space=pl.ANY)


def plan_kernel(sub_ref, hid_ref, ext_ref, rank_ref, off_ref):
    ids = iota((ADAPTERS, ROWS), 0)
    chosen = jnp.zeros((ADAPTERS, ROWS), F32)
    for k in range(sub_ref.shape[0]):
        chosen = chosen + jnp.where(sub_ref[k : k + 1, :] == ids, 1.0, 0.0)
    named = chosen.astype(BF16)
    earlier = jnp.where(iota((ROWS, ROWS), 0) < iota((ROWS, ROWS), 1), 1.0, 0.0)
    before = dot(named, earlier.astype(BF16), 1, 0)
    rank = jnp.where(chosen > 0.5, before, -1.0)
    rank_ref[...] = rank
    ext_ref[0:ROWS, :] = hid_ref[...]
    ext_ref[ROWS:, 0:ROWS] = rank.astype(BF16)
    ext_ref[ROWS:, ROWS:] = jnp.zeros((ADAPTERS, WIDTH - ROWS), BF16)
    count = jnp.sum(chosen, axis=1, keepdims=True)
    padded = jnp.broadcast_to(jnp.floor((count + (TILE - 1)) * (1.0 / TILE)) * TILE, (ADAPTERS, 128))
    lower = jnp.where(iota((ADAPTERS, ADAPTERS), 1) < iota((ADAPTERS, ADAPTERS), 0), 1.0, 0.0)
    off_ref[...] = dot(lower.astype(BF16), padded.astype(BF16), 1, 0).astype(jnp.int32)


def plan(subsets, hidden):
    return pl.pallas_call(
        plan_kernel,
        out_shape=(
            jax.ShapeDtypeStruct((ROWS + ADAPTERS, WIDTH), BF16),
            jax.ShapeDtypeStruct((ADAPTERS, ROWS), F32),
            jax.ShapeDtypeStruct((ADAPTERS, 128), jnp.int32),
        ),
        in_specs=[whole(), whole()],
        out_specs=(whole(), whole(), whole()),
        compiler_params=params(),
        name="plan",
    )(subsets.T, hidden)


def spread_kernel(rank_ref, pick_ref):
    rest = jnp.full((CAP - ADAPTERS, ROWS), -1.0, F32)
    cols = jnp.concatenate([rank_ref[...], rest], axis=0).T.astype(BF16)
    slots = iota((ROWS, CAP), 1).astype(F32)
    for a in range(ADAPTERS):
        one = jnp.where(iota((CAP, CAP), 0) == a, 1.0, 0.0).astype(BF16)
        pick_ref[:, a * CAP : (a + 1) * CAP] = jnp.where(dot(cols, one, 1, 0) == slots, 1.0, 0.0).astype(BF16)


def spread(rank):
    return pl.pallas_call(
        spread_kernel,
        out_shape=jax.ShapeDtypeStruct((ROWS, ADAPTERS * CAP), BF16),
        in_specs=[whole()],
        out_specs=whole(),
        compiler_params=params(),
        name="spread",
    )(rank)


def block_copies(pos_ref, weight_ref, held, sems, sign):
    copies = []
    for s in range(4):
        p = (pos_ref[3] + (s if sign > 0 else 4 - s)) & 3
        cols = pl.ds(pl.multiple_of(p * WIDTH, WIDTH), WIDTH)
        copies.append(pltpu.make_async_copy(weight_ref.at[:, cols], held.at[s], sems.at[s]))
    for s in (2, 1, 3, 0):
        copies[s].start()
    return copies


def query_kernel(pos_ref, ext_ref, weight_ref, *refs):
    outs, held, sems = refs[:4], refs[4], refs[5]
    copies = block_copies(pos_ref, weight_ref, held, sems, 1)
    for s in (2, 1, 3, 0):
        copies[s].wait()
        outs[s][...] = dot(ext_ref[0:ROWS, :], held[s], 1, 0).astype(BF16)


def query_parts(pos, ext, weight):
    return pl.pallas_call(
        query_kernel,
        out_shape=[jax.ShapeDtypeStruct((ROWS, WIDTH), BF16)] * 4,
        in_specs=[smem(), whole(), anywhere()],
        out_specs=[whole()] * 4,
        scratch_shapes=[pltpu.VMEM((4, WIDTH, WIDTH), BF16), pltpu.SemaphoreType.DMA((4,))],
        compiler_params=params(),
        name="query_parts",
    )(pos, ext, weight)


def probe_kernel(pos_ref, q0, q1, q2, q3, hid_ref, weight_ref, probe_ref, own_ref, held, sems):
    copies = block_copies(pos_ref, weight_ref, held, sems, -1)
    total = jnp.zeros((ROWS, WIDTH), F32)
    for s, q in ((2, q2), (1, q1), (3, q3), (0, q0)):
        copies[s].wait()
        total = total + dot(q[...], held[s], 1, 1)
    probe = total.astype(BF16)
    probe_ref[...] = probe
    own = jnp.sum(probe.astype(F32) * hid_ref[...].astype(F32), axis=1, keepdims=True)
    own_ref[...] = jnp.broadcast_to(own, (ROWS, 128)).T[0:8, :]


def probe_of(pos, query, weight, hidden):
    return pl.pallas_call(
        probe_kernel,
        out_shape=(
            jax.ShapeDtypeStruct((ROWS, WIDTH), BF16),
            jax.ShapeDtypeStruct((8, ROWS), F32),
        ),
        in_specs=[smem()] + [whole()] * 5 + [anywhere()],
        out_specs=(whole(), whole()),
        scratch_shapes=[pltpu.VMEM((4, WIDTH, WIDTH), BF16), pltpu.SemaphoreType.DMA((4,))],
        compiler_params=params(),
        name="probe",
    )(pos, *query, hidden, weight)


def adapter_of(pos_ref, sx, i):
    return (i // 2 * 4 + ((pos_ref[1] + (4 - sx)) & 3)) * 2 + i % 2


def squeeze_kernel(pos_ref, *refs):
    exts, weights, outs = refs[:4], refs[4], refs[5:9]
    rows, ranks, held, row_sems, rank_sems, sems = refs[9:]
    row_copies, rank_copies = [], []
    for s in range(4):
        some = pl.ds(s * ROWS, ROWS)
        row_copies.append(pltpu.make_async_copy(exts[s].at[pl.ds(0, ROWS)], rows.at[some], row_sems.at[s]))
        rest = exts[s].at[pl.ds(ROWS, ADAPTERS), pl.ds(0, ROWS)]
        rank_copies.append(pltpu.make_async_copy(rest, ranks.at[s], rank_sems.at[s]))
    copies = [
        pltpu.make_async_copy(weights.at[i], held.at[:, pl.ds(i * B, B)], sems.at[i]) for i in range(8)
    ]
    for copy in row_copies + copies[:4] + rank_copies + copies[4:]:
        copy.start()
    ids = iota((ADAPTERS, ROWS), 0)
    slots = iota((CAP, ROWS), 0).astype(F32)
    for copy in row_copies:
        copy.wait()
    for j in range(2):
        for i in range(4 * j, 4 * j + 4):
            copies[i].wait()
        part = dot(rows[...], held[:, 4 * j * B : 4 * (j + 1) * B], 1, 0).astype(BF16)
        if j == 0:
            for copy in rank_copies:
                copy.wait()
        for i in range(4 * j, 4 * j + 4):
            a = adapter_of(pos_ref, 0, i)
            cols = slice((i - 4 * j) * B, (i - 4 * j + 1) * B)
            for s in range(4):
                mine = jnp.sum(jnp.where(ids == a, ranks[s].astype(F32), 0.0), axis=0, keepdims=True)
                pick = jnp.where(slots == mine, 1.0, 0.0).astype(BF16)
                outs[s][i] = dot(pick, part[s * ROWS : (s + 1) * ROWS, cols], 1, 0).astype(BF16)


def squeeze(pos, exts, weights):
    return pl.pallas_call(
        squeeze_kernel,
        out_shape=[jax.ShapeDtypeStruct((8, CAP, B), BF16)] * 4,
        in_specs=[smem()] + [anywhere()] * 5,
        out_specs=[whole()] * 4,
        scratch_shapes=[
            pltpu.VMEM((4 * ROWS, WIDTH), BF16),
            pltpu.VMEM((4, ADAPTERS, ROWS), BF16),
            pltpu.VMEM((WIDTH, 8 * B), BF16),
            pltpu.SemaphoreType.DMA((4,)),
            pltpu.SemaphoreType.DMA((4,)),
            pltpu.SemaphoreType.DMA((8,)),
        ],
        compiler_params=params(),
        name="squeeze",
    )(pos, *exts, weights)


def pack_kernel(pos_ref, off_ref, *refs):
    blocks, outs, buf = refs[:4], refs[4:8], refs[8]
    buf[...] = jnp.zeros_like(buf)
    for t in range(4):
        for i in range(8):
            a = adapter_of(pos_ref, t, i)
            at = pl.ds(pl.multiple_of(off_ref[a], TILE), CAP)
            buf[at, :] = buf[at, :] + blocks[t][i]
    for s in range(4):
        p = (pos_ref[3] + s) & 3
        outs[s][...] = buf[pl.ds(pl.multiple_of(p * PIECE, TILE), PIECE), :]


def pack(pos, off, blocks):
    return pl.pallas_call(
        pack_kernel,
        out_shape=[jax.ShapeDtypeStruct((PIECE, B), BF16)] * 4,
        in_specs=[pl.BlockSpec(memory_space=pltpu.SMEM)] * 2 + [whole()] * 4,
        out_specs=[whole()] * 4,
        scratch_shapes=[pltpu.VMEM((BUF, B), BF16)],
        compiler_params=params(),
        name="pack",
    )(pos, off, *blocks)


def unpack_into(buf, pos_ref, pieces):
    for s in range(4):
        p = (pos_ref[3] + (4 - s)) & 3
        buf[pl.ds(pl.multiple_of(p * PIECE, TILE), PIECE), :] = pieces[s][...]
    buf[PAIRS:, :] = jnp.zeros((CAP, B), BF16)


PER = 4
STEPS = ADAPTERS // PER
ORDER = list(range(ADAPTERS))


def step_copies(up_ref, held, bottle_ref, bottles, sems):
    copies = []
    for g in range(STEPS):
        some = pl.ds(g * PER, PER)
        cols = pl.ds(g * PER * B, PER * B)
        copies.append(
            (
                pltpu.make_async_copy(bottle_ref.at[:, cols], bottles.at[:, cols], sems.at[0, g]),
                pltpu.make_async_copy(up_ref.at[some], held.at[some], sems.at[1, g]),
            )
        )
        for copy in copies[g]:
            copy.start()

    def arrive(g):
        for copy in copies[g]:
            copy.wait()

    return arrive


def segment(buf, off_ref, a):
    return buf[pl.ds(pl.multiple_of(off_ref[a], TILE), CAP), :]


def expand_kernel(pos_ref, off_ref, g0, g1, g2, g3, pick_ref, out_ref, buf):
    unpack_into(buf, pos_ref, (g0, g1, g2, g3))
    for i, a in enumerate(ORDER):
        pick = pick_ref[:, a * CAP : (a + 1) * CAP]
        out_ref[:, i * B : (i + 1) * B] = dot(pick, segment(buf, off_ref, a), 1, 0).astype(BF16)


def expand(pos, off, pieces, pick):
    return pl.pallas_call(
        expand_kernel,
        out_shape=jax.ShapeDtypeStruct((ROWS, ADAPTERS * B), BF16),
        in_specs=[smem(), smem()] + [whole()] * 5,
        out_specs=whole(),
        scratch_shapes=[pltpu.VMEM((BUF, B), BF16)],
        compiler_params=params(24 * 1024 * 1024),
        name="expand",
    )(pos, off, *pieces, pick)


def logits_kernel(bottle_ref, probe_ref, own_ref, up_ref, out_ref, held, bottles, sems):
    arrive = step_copies(up_ref, held, bottle_ref, bottles, sems)
    out_ref[ADAPTERS:, :] = own_ref[...]
    lane = iota((ROWS, 128), 1)
    found = jnp.zeros((ROWS, 128), F32)
    turned = None
    for g in range(STEPS + 1):
        before = turned
        if g < STEPS:
            arrive(g)
            turned = dot(probe_ref[...], held[g * PER : (g + 1) * PER].reshape(PER * B, WIDTH), 1, 1)
        for i in range((g - 1) * PER, g * PER) if g else ():
            k = i % PER
            bottle = bottles[:, i * B : (i + 1) * B].astype(F32)
            logit = jnp.sum(before[:, k * B : (k + 1) * B] * bottle, axis=1, keepdims=True)
            found = jnp.where(lane == ORDER[i], logit, found)
    out_ref[0:ADAPTERS, :] = found.T[0:ADAPTERS, :]


LESS = 48 * 1024 * 1024


def logits_of(bottle, probe, own, up):
    return pl.pallas_call(
        logits_kernel,
        out_shape=jax.ShapeDtypeStruct((ADAPTERS + 8, ROWS), F32),
        in_specs=[anywhere()] + [whole()] * 2 + [anywhere()],
        out_specs=whole(),
        scratch_shapes=[
            pltpu.VMEM((ADAPTERS, B, WIDTH), BF16),
            pltpu.VMEM((ROWS, ADAPTERS * B), BF16),
            pltpu.SemaphoreType.DMA((2, STEPS)),
        ],
        compiler_params=params(),
        name="logits",
    )(bottle, probe, own, up)


def join_kernel(bottles, l0, l1, l2, l3, rank_ref, hid_ref, up_ref, out_ref, held, sems):
    copies = []
    for g in range(STEPS):
        some = pl.ds(g * PER, PER)
        copies.append(pltpu.make_async_copy(up_ref.at[some], held.at[some], sems.at[g]))
        copies[g].start()
    total = (l0[...] + l1[...]) + (l2[...] + l3[...])
    logits = (total[0:ADAPTERS] + total[ADAPTERS : ADAPTERS + 1]) * D ** (-0.5)
    chosen = rank_ref[...] >= 0.0
    logits = jnp.where(chosen, logits, -jnp.inf)
    e = jnp.where(chosen, jnp.exp(logits - jnp.max(logits, axis=0, keepdims=True)), 0.0)
    share = e / jnp.sum(e, axis=0, keepdims=True)
    share = jnp.concatenate([share, jnp.zeros((128 - ADAPTERS, ROWS), F32)], axis=0).T
    total = hid_ref[...].astype(F32)
    for g in range(STEPS):
        mix = []
        for i in range(g * PER, (g + 1) * PER):
            a = ORDER[i]
            bottle = bottles[:, i * B : (i + 1) * B].astype(F32)
            mix.append((bottle * share[:, a : a + 1]).astype(BF16))
        copies[g].wait()
        up = held[g * PER : (g + 1) * PER].reshape(PER * B, WIDTH)
        total = total + dot(jnp.concatenate(mix, axis=1), up, 1, 0)
    out_ref[...] = total.astype(BF16)


def join(bottle, parts, rank, hidden, up):
    return pl.pallas_call(
        join_kernel,
        out_shape=jax.ShapeDtypeStruct((ROWS, WIDTH), BF16),
        in_specs=[whole()] * 7 + [anywhere()],
        out_specs=whole(),
        scratch_shapes=[
            pltpu.VMEM((ADAPTERS, B, WIDTH), BF16),
            pltpu.SemaphoreType.DMA((STEPS,)),
        ],
        compiler_params=params(LESS),
        name="join",
    )(bottle, *parts, rank, hidden, up)


def shifted(x, axis, s):
    return lax.ppermute(x, axis, [(i, (i + s) % 4) for i in range(4)])


def round_trip(x, axis):
    return [x] + [shifted(x, axis, s) for s in (1, 2, 3)]


def gathered(xs, axis):
    return [xs[0]] + [shifted(xs[s], axis, s) for s in (1, 2, 3)]


def summed(xs):
    xs = [x.astype(F32) for x in xs]
    return (xs[0] + xs[1]) + (xs[2] + xs[3])


def per_device(hidden, subsets, down_weight, up_weight, query_weight, key_weight):
    pos = jnp.stack([lax.axis_index(n) for n in ("y", "x", "core", "mp")]).astype(jnp.int32)
    ext, rank, off = plan(subsets, hidden)
    pick = spread(rank)
    off = off[:, 0]

    parts = query_parts(pos, ext, query_weight)
    downs = lax.all_gather(down_weight, ("y", "core"), axis=0, tiled=True)
    exts = round_trip(ext, "x")
    near = [parts[0]] + [shifted(parts[s], "mp", s) for s in (1, 3)]
    phase = (exts, downs, near, parts[2], pick, up_weight)
    exts, downs, near, far, pick, up_weight = lax.optimization_barrier(phase)
    parts = near + [shifted(far, "mp", 2)]

    up = lax.all_gather(up_weight, ("y", "x", "core"), axis=0, tiled=True)
    made = squeeze(pos, exts, downs)
    back = gathered([made[0], made[3], made[2], made[1]], "x")
    query = summed(parts).astype(BF16)
    query = round_trip(query, "mp")

    sent = pack(pos, off, back)
    probe, own = probe_of(pos, query, key_weight, hidden)
    got = gathered(sent, "mp")
    got, probe = lax.optimization_barrier((got, probe))
    pieces = round_trip(jnp.maximum(summed(got), 0.0).astype(BF16), "mp")

    bottle = expand(pos, off, pieces, pick)
    partial = logits_of(bottle, probe, own, up)
    partials = round_trip(partial, "mp")
    return join(bottle, partials, rank, hidden, up)


def solution(mesh):
    split = Mesh(mesh.devices.reshape(4, 4, 2, 4), ("y", "x", "core", "mp"))
    rows = ("y", "x", "core")
    return jax.shard_map(
        per_device,
        mesh=split,
        in_specs=(
            P(rows, "mp"),
            P(rows, None),
            P(rows, "mp", None),
            P(rows, None, "mp"),
            P("mp", None),
            P("mp", None),
        ),
        out_specs=P(rows, "mp"),
        check_vma=False,
    )
```
